32 devices in a mesh: fsdp: 4 (over z), cp: 2 (over core), tp: 4 (over y, x).
Axes of the slice: x: 2, y: 2, z: 4, core: 2. Of those that a mesh axis runs over, the one named last changes fastest.
Arguments:
- tokens: bfloat16 [4096, 1024], P(('fsdp', 'cp', 'tp')), may hold values from -6 to 6
- cotangent: bfloat16 [4096, 1024], P(('fsdp', 'cp', 'tp')), may hold values from -6 to 6
- counts: int32 [4, 2], P('fsdp'), may hold values from 384 to 512, as said below
- lengths: int32 [4, 4], P('fsdp'), may hold values from 1 to 512, 896 in all within a row
- attn_gain: bfloat16 [1024], P(('fsdp', 'cp')), may hold values from 0.25 to 1.75
- w_q: bfloat16 [1024, 2048], P(('fsdp', 'cp'), 'tp'), may hold values from -0.1875 to 0.1875
- key_matrix: bfloat16 [1024, 1024], P(('fsdp', 'cp'), 'tp'), may hold values from -0.1875 to 0.1875
- value_matrix: bfloat16 [1024, 1024], P(('fsdp', 'cp'), 'tp'), may hold values from -0.1875 to 0.1875
- q_gain: bfloat16 [128], P(('fsdp', 'cp')), may hold values from 0.25 to 1.75
- k_gain: bfloat16 [128], P(('fsdp', 'cp')), may hold values from 0.25 to 1.75
- w_o: bfloat16 [1024, 2048], P(('fsdp', 'cp'), 'tp'), may hold values from -0.5 to 0.5
- mlp_gain: bfloat16 [1024], P(('fsdp', 'cp')), may hold values from 0.25 to 1.75
- w_gate: bfloat16 [1024, 3072], P(('fsdp', 'cp'), 'tp'), may hold values from -0.1875 to 0.1875
- w_up: bfloat16 [1024, 3072], P(('fsdp', 'cp'), 'tp'), may hold values from -0.1875 to 0.1875
- w_down: bfloat16 [1024, 3072], P(('fsdp', 'cp'), 'tp'), may hold values from -0.109375 to 0.109375
Outputs:
- out: bfloat16 [4096, 1024], P(('fsdp', 'cp', 'tp'))
- d_input: float32 [4096, 1024], P(('fsdp', 'cp', 'tp'))
- grad_attn_gain: float32 [1024], P(('fsdp', 'cp'))
- grad_w_q: float32 [1024, 2048], P(('fsdp', 'cp'), 'tp')
- grad_w_k: float32 [1024, 1024], P(('fsdp', 'cp'), 'tp')
- grad_w_v: float32 [1024, 1024], P(('fsdp', 'cp'), 'tp')
- grad_q_gain: float32 [128], P(('fsdp', 'cp'))
- grad_k_gain: float32 [128], P(('fsdp', 'cp'))
- grad_w_o: float32 [1024, 2048], P(('fsdp', 'cp'), 'tp')
- grad_mlp_gain: float32 [1024], P(('fsdp', 'cp'))
- grad_w_gate: float32 [1024, 3072], P(('fsdp', 'cp'), 'tp')
- grad_w_up: float32 [1024, 3072], P(('fsdp', 'cp'), 'tp')
- grad_w_down: float32 [1024, 3072], P(('fsdp', 'cp'), 'tp')
The draws below stay inside these ranges and needn't reach their ends.
Inputs may be any that keep to these rules, and one draw needn't show every extreme that they name: Each row of counts sums to 896; pack f's tokens in order are the live slots of its block 0, then those of its block 1; some block of every draw has all 512 slots live. Each row of lengths sums to 896 and holds one sequence of exactly 512 tokens.
All inputs are finite; a program needn't handle non-finite values.
Results may differ from the reference program's by a relative error of at most 0.014.
Values may be sent and summed in bfloat16 or wider, within the bound.
No kernel may reach another device: no remote copies, remote signals or barrier semaphores. Data moves between devices by JAX's collectives and lax.ppermute only.
A program may use at most 128 MiB of HBM per device.

```python
import math
import jax
import jax.numpy as jnp
import numpy as np
from jax import lax

MODEL_WIDTH = 1024
QUERY_HEADS = 16
KEY_VALUE_HEADS = 8
HEAD_SIZE = 128
FF = 3072
CAP = 512
NSEQ = 4
PACK = 896
SEQMAX = 512
ROWS = 4096
N_FSDP = 4


def draw_counts(key, part):
    key_fill, key_row, key_swap = jax.random.split(key, 3)
    first_block = jax.random.randint(key_fill, (N_FSDP,), PACK - CAP, CAP + 1, dtype=jnp.int32)
    chosen = jax.random.randint(key_row, (), 0, N_FSDP, dtype=jnp.int32)
    first_block = jnp.where(jnp.arange(N_FSDP, dtype=jnp.int32) == chosen, CAP, first_block).astype(jnp.int32)
    swapped = jax.random.randint(key_swap, (N_FSDP,), 0, 2, dtype=jnp.int32)
    second = (PACK - first_block).astype(jnp.int32)
    left_count = jnp.where(swapped == 1, second, first_block)
    right_count = jnp.where(swapped == 1, first_block, second)
    return jnp.stack([left_count, right_count], axis=1).astype(jnp.int32)


def block_scale(own_key, extent, pieces, smallest, largest):
    factor_of, own = 1.0, jax.random.fold_in(own_key, 6)
    for position, parts in pieces:
        draws = jnp.exp(jax.random.uniform(jax.random.fold_in(own, position), (parts,), jnp.float32, smallest / len(pieces), largest / len(pieces)))
        factor_of = factor_of * jnp.repeat(draws, extent[position] // parts).reshape([-1 if axis == position else 1 for axis in range(len(extent))])
    return factor_of


def split_up(amount, total, limit, lean):
    portions = [(1 << 20) // math.isqrt(grade ** lean) + 1 for grade in range(2, amount + 1)]
    spare, holding = total - limit - (amount - 1), [1] * (amount - 1)
    while spare > 0:
        free = [i for i in range(amount - 1) if holding[i] < limit]
        whole, left = sum([portions[i] for i in free]), spare
        for i in free:
            more = min(limit - holding[i], max(1, left * portions[i] // whole), spare)
            holding[i] = holding[i] + more
            spare = spare - more
    return np.array([limit] + holding)


def ragged(own_key, amount, total, most, slope):
    if amount == 2:
        one = jax.random.randint(own_key, (), max(1, total - most), min(most, total - 1) + 1)
        return jnp.stack([one, total - one])
    sizes = jnp.asarray(split_up(amount, total, most, slope), jnp.int32)
    couples = (amount - 1) // 2
    giver, taker = sizes[1:1 + 2 * couples:2], sizes[2:2 + 2 * couples:2]
    margin = jnp.minimum(giver - 1, most - taker)
    moved = jax.random.randint(jax.random.fold_in(own_key, 1), (couples,), 0, 1 << 20) % (margin + 1)
    sizes = sizes.at[1:1 + 2 * couples:2].set(giver - moved).at[2:2 + 2 * couples:2].set(taker + moved)
    return sizes[jax.random.permutation(jax.random.fold_in(own_key, 2), amount)]


def gaussian(stream_key, dims, scale, bound, cuts=(), held_as=jnp.bfloat16):
    entries = scale * jax.random.normal(stream_key, dims, jnp.float32)
    if cuts:
        entries = entries * block_scale(stream_key, dims, cuts, -0.22, 0.18)
    return jnp.clip(entries, -bound, bound).astype(held_as)


def setup_inputs(seed: int = 0) -> dict:
    key_list = jax.random.split(jax.random.key(seed), 16)
    tokens = gaussian(key_list[0], (ROWS, MODEL_WIDTH), 1.0, 6.0, ((0, 32),))
    cotangent = gaussian(key_list[1], (ROWS, MODEL_WIDTH), 1.0, 6.0, ((0, 32),))
    counts = draw_counts(jax.random.fold_in(key_list[15], 71), 0)
    lengths = jax.vmap(lambda own: ragged(own, NSEQ, PACK, SEQMAX, 2))(jax.random.split(key_list[3], N_FSDP)).reshape((N_FSDP, NSEQ)).astype(jnp.int32)
    attn_gain = jnp.clip(1.0 + 0.15 * jax.random.normal(key_list[4], (MODEL_WIDTH,), jnp.float32), 0.25, 1.75).astype(jnp.bfloat16)
    w_q = gaussian(key_list[5], (MODEL_WIDTH, QUERY_HEADS * HEAD_SIZE), MODEL_WIDTH ** -0.5, 0.1875, ((0, 8), (1, 4)))
    key_matrix = gaussian(key_list[6], (MODEL_WIDTH, KEY_VALUE_HEADS * HEAD_SIZE), MODEL_WIDTH ** -0.5, 0.1875, ((0, 8), (1, 4)))
    value_matrix = gaussian(key_list[7], (MODEL_WIDTH, KEY_VALUE_HEADS * HEAD_SIZE), MODEL_WIDTH ** -0.5, 0.1875, ((0, 8), (1, 4)))
    q_gain = jnp.clip(1.0 + 0.15 * jax.random.normal(key_list[8], (HEAD_SIZE,), jnp.float32), 0.25, 1.75).astype(jnp.bfloat16)
    k_gain = jnp.clip(1.0 + 0.15 * jax.random.normal(key_list[9], (HEAD_SIZE,), jnp.float32), 0.25, 1.75).astype(jnp.bfloat16)
    w_o = gaussian(key_list[10], (MODEL_WIDTH, QUERY_HEADS * HEAD_SIZE), (QUERY_HEADS * HEAD_SIZE // 16) ** -0.5, 0.5, ((0, 8), (1, 4)))
    mlp_gain = jnp.clip(1.0 + 0.15 * jax.random.normal(key_list[11], (MODEL_WIDTH,), jnp.float32), 0.25, 1.75).astype(jnp.bfloat16)
    w_gate = gaussian(key_list[12], (MODEL_WIDTH, FF), MODEL_WIDTH ** -0.5, 0.1875, ((0, 8), (1, 4)))
    w_up = gaussian(key_list[13], (MODEL_WIDTH, FF), MODEL_WIDTH ** -0.5, 0.1875, ((0, 8), (1, 4)))
    w_down = gaussian(key_list[14], (MODEL_WIDTH, FF), FF ** -0.5, 0.109375, ((0, 8), (1, 4)))
    return {"tokens": tokens, "cotangent": cotangent, "counts": counts, "lengths": lengths, "attn_gain": attn_gain, "w_q": w_q, "key_matrix": key_matrix, "value_matrix": value_matrix, "q_gain": q_gain, "k_gain": k_gain, "w_o": w_o, "mlp_gain": mlp_gain, "w_gate": w_gate, "w_up": w_up, "w_down": w_down}


EPS = 1e-06
THETA = 1000000.0

def rms_scale(value_tensor):
    return lax.rsqrt(lax.optimization_barrier(jnp.mean(value_tensor * value_tensor, axis=-1, keepdims=True)) + EPS)

def contract_last(left, right):
    return lax.dot_general(left, right, (((1,), (1,)), ((), ())), preferred_element_type=jnp.float32)

def contract_first(left, right):
    return lax.dot_general(left, right, (((0,), (0,)), ((), ())), preferred_element_type=jnp.float32)

def pack_layout(counts_row, lengths_row, block_rows):
    row_index = jnp.arange(2 * block_rows, dtype=jnp.int32)
    in_second = row_index >= block_rows
    within = (row_index - jnp.where(in_second, block_rows, 0)).astype(jnp.int32)
    live_rows = within < jnp.where(in_second, counts_row[1], counts_row[0])
    pack_pos = (within + jnp.where(in_second, counts_row[0], 0)).astype(jnp.int32)
    bounds = jnp.cumsum(lengths_row).astype(jnp.int32)
    seq_id = lax.optimization_barrier(jnp.sum((bounds[None, :] <= pack_pos[:, None]).astype(jnp.int32), axis=1)).astype(jnp.int32)
    seq_order = jnp.arange(lengths_row.shape[0], dtype=jnp.int32)
    before = lax.optimization_barrier(jnp.sum(jnp.where(seq_order[None, :] < seq_id[:, None], lengths_row[None, :], 0), axis=1)).astype(jnp.int32)
    return (live_rows, pack_pos, seq_id, (pack_pos - before).astype(jnp.int32))

def attend_mask(live_rows, pack_pos, seq_id):
    row_index = jnp.arange(live_rows.shape[0], dtype=jnp.int32)
    same_seq = (seq_id[:, None] == seq_id[None, :]) & (pack_pos[None, :] <= pack_pos[:, None])
    joint = live_rows[:, None] & live_rows[None, :] & same_seq
    return joint | (row_index[:, None] == row_index[None, :]) & jnp.logical_not(live_rows)[:, None]

def rotary(positions, width):
    half_width = width // 2
    frequency = THETA ** (-2.0 * jnp.arange(half_width, dtype=jnp.float32) / width)
    angles = positions.astype(jnp.float32)[:, None] * frequency[None, :]
    return (jnp.cos(angles)[:, None, :], jnp.sin(angles)[:, None, :])

def rotate(value_tensor, cosine, sine):
    half_width = value_tensor.shape[-1] // 2
    first_half = value_tensor[..., :half_width]
    second = value_tensor[..., half_width:]
    return jnp.concatenate([first_half * cosine - second * sine, second * cosine + first_half * sine], axis=-1)

def head_norm(raw_values, gain_values, cosine, sine):
    return rotate(raw_values * rms_scale(raw_values) * gain_values, cosine, sine)

def head_norm_back(raw_values, gain_values, cosine, sine, grad_rot):
    row_scale = rms_scale(raw_values)
    unit_values = raw_values * row_scale
    grad_norm = rotate(grad_rot, cosine, -sine)
    gain_grad = lax.optimization_barrier(jnp.sum(grad_norm * unit_values, axis=(0, 1)))
    scaled = grad_norm * gain_values
    grad_raw = row_scale * (scaled - unit_values * lax.optimization_barrier(jnp.mean(scaled * unit_values, axis=-1, keepdims=True)))
    return (grad_raw, gain_grad)

def row_norm_back(value_tensor, gain_values, grad_out):
    row_scale = rms_scale(value_tensor)
    unit_values = value_tensor * row_scale
    gain_grad = lax.optimization_barrier(jnp.sum(grad_out * unit_values, axis=0))
    scaled = grad_out * gain_values
    grad_values = row_scale * (scaled - unit_values * lax.optimization_barrier(jnp.mean(scaled * unit_values, axis=-1, keepdims=True)))
    return (grad_values, gain_grad)

def layer_group(rows_in, cot_in, counts_row, lengths_row, params):
    attn_gain, w_q, key_matrix, value_matrix, q_gain, k_gain, w_o, mlp_gain, w_gate, w_up, w_down = params
    grouped_query_rows = rows_in.shape[0]
    live_rows, pack_pos, seq_id, positions = pack_layout(counts_row, lengths_row, grouped_query_rows // 2)
    allowed = attend_mask(live_rows, pack_pos, seq_id)
    mask_rows = live_rows.astype(jnp.float32)[:, None]
    inputs = rows_in.astype(jnp.float32) * mask_rows
    first_normalized = (inputs * rms_scale(inputs) * attn_gain.astype(jnp.float32)).astype(jnp.bfloat16)
    query_raw = jnp.dot(first_normalized, w_q, preferred_element_type=jnp.float32).reshape(grouped_query_rows, QUERY_HEADS, HEAD_SIZE)
    unrotated_key = jnp.dot(first_normalized, key_matrix, preferred_element_type=jnp.float32).reshape(grouped_query_rows, KEY_VALUE_HEADS, HEAD_SIZE)
    value_tensor = jnp.dot(first_normalized, value_matrix, preferred_element_type=jnp.float32).astype(jnp.bfloat16).reshape(grouped_query_rows, KEY_VALUE_HEADS, HEAD_SIZE)
    cosine, sine = rotary(positions, HEAD_SIZE)
    queries = head_norm(query_raw, q_gain.astype(jnp.float32), cosine, sine).astype(jnp.bfloat16)
    key_rows = head_norm(unrotated_key, k_gain.astype(jnp.float32), cosine, sine).astype(jnp.bfloat16)
    queries_per_group = QUERY_HEADS // KEY_VALUE_HEADS
    key_wide = jnp.repeat(key_rows, queries_per_group, axis=1).astype(jnp.float32)
    value_wide = jnp.repeat(value_tensor, queries_per_group, axis=1).astype(jnp.float32)
    factor = HEAD_SIZE ** (-0.5)
    scores = jnp.einsum('qhd,khd->hqk', queries.astype(jnp.float32), key_wide) * factor
    scores = jnp.where(allowed[None], scores, -jnp.inf)
    top_score = lax.optimization_barrier(jnp.max(scores, axis=2, keepdims=True))
    log_total = top_score + jnp.log(lax.optimization_barrier(jnp.sum(jnp.exp(scores - top_score), axis=2, keepdims=True)))
    probs = jnp.exp(scores - log_total)
    probs_low = probs.astype(jnp.bfloat16)
    mixed_heads = jnp.einsum('hqk,khd->qhd', probs_low.astype(jnp.float32), value_wide).astype(jnp.bfloat16)
    mixed_flat = mixed_heads.reshape(grouped_query_rows, QUERY_HEADS * HEAD_SIZE)
    residual = inputs + contract_last(mixed_flat, w_o)
    normed_two = (residual * rms_scale(residual) * mlp_gain.astype(jnp.float32)).astype(jnp.bfloat16)
    gate_val = jnp.dot(normed_two, w_gate, preferred_element_type=jnp.float32)
    up_val = jnp.dot(normed_two, w_up, preferred_element_type=jnp.float32)
    sigmoid_gate = jax.nn.sigmoid(gate_val)
    hidden = (gate_val * sigmoid_gate * up_val).astype(jnp.bfloat16)
    output = (residual + contract_last(hidden, w_down)).astype(jnp.bfloat16)
    cot_live = cot_in.astype(jnp.float32) * mask_rows
    cot_low = cot_live.astype(jnp.bfloat16)
    grad_hidden = jnp.dot(cot_low, w_down, preferred_element_type=jnp.float32)
    grad_down = contract_first(cot_low, hidden)
    grad_gate_val = (grad_hidden * up_val * sigmoid_gate * (1.0 + gate_val * (1.0 - sigmoid_gate))).astype(jnp.bfloat16)
    grad_up_val = (grad_hidden * gate_val * sigmoid_gate).astype(jnp.bfloat16)
    grad_gate = contract_first(normed_two, grad_gate_val)
    grad_up = contract_first(normed_two, grad_up_val)
    grad_normed_two = contract_last(grad_gate_val, w_gate) + contract_last(grad_up_val, w_up)
    grad_resid_norm, grad_mlp = row_norm_back(residual, mlp_gain.astype(jnp.float32), grad_normed_two)
    grad_resid = cot_live + grad_resid_norm
    resid_low = grad_resid.astype(jnp.bfloat16)
    grad_out = contract_first(resid_low, mixed_flat)
    grad_mixed = jnp.dot(resid_low, w_o, preferred_element_type=jnp.float32).astype(jnp.bfloat16).reshape(grouped_query_rows, QUERY_HEADS, HEAD_SIZE)
    row_delta = lax.optimization_barrier(jnp.sum(grad_mixed.astype(jnp.float32) * mixed_heads.astype(jnp.float32), axis=2)).T[:, :, None]
    grad_probs = jnp.einsum('qhd,khd->hqk', grad_mixed.astype(jnp.float32), value_wide)
    grad_scores = (probs * (grad_probs - row_delta)).astype(jnp.bfloat16).astype(jnp.float32)
    expanded_value_gradient = jnp.einsum('hqk,qhd->khd', probs_low.astype(jnp.float32), grad_mixed.astype(jnp.float32))
    grad_query = (jnp.einsum('hqk,khd->qhd', grad_scores, key_wide) * factor).astype(jnp.bfloat16)
    expanded_key_gradient = jnp.einsum('hqk,qhd->khd', grad_scores, queries.astype(jnp.float32)) * factor
    key_gradient = lax.optimization_barrier(jnp.sum(expanded_key_gradient.reshape(grouped_query_rows, KEY_VALUE_HEADS, queries_per_group, HEAD_SIZE), axis=2)).astype(jnp.bfloat16)
    value_gradient = lax.optimization_barrier(jnp.sum(expanded_value_gradient.reshape(grouped_query_rows, KEY_VALUE_HEADS, queries_per_group, HEAD_SIZE), axis=2)).astype(jnp.bfloat16)
    grad_query_raw, grad_qgain = head_norm_back(query_raw, q_gain.astype(jnp.float32), cosine, sine, grad_query.astype(jnp.float32))
    unrotated_key_gradient, grad_kgain = head_norm_back(unrotated_key, k_gain.astype(jnp.float32), cosine, sine, key_gradient.astype(jnp.float32))
    query_back = grad_query_raw.astype(jnp.bfloat16).reshape(grouped_query_rows, QUERY_HEADS * HEAD_SIZE)
    key_reverse_pass = unrotated_key_gradient.astype(jnp.bfloat16).reshape(grouped_query_rows, KEY_VALUE_HEADS * HEAD_SIZE)
    value_reverse_pass = value_gradient.reshape(grouped_query_rows, KEY_VALUE_HEADS * HEAD_SIZE)
    grad_wq = contract_first(first_normalized, query_back)
    grad_wk = contract_first(first_normalized, key_reverse_pass)
    grad_wv = contract_first(first_normalized, value_reverse_pass)
    grad_normed_one = contract_last(query_back, w_q) + contract_last(key_reverse_pass, key_matrix) + contract_last(value_reverse_pass, value_matrix)
    grad_inputs_norm, grad_attn = row_norm_back(inputs, attn_gain.astype(jnp.float32), grad_normed_one)
    grad_inputs = (grad_resid + grad_inputs_norm) * mask_rows
    grads = (grad_attn, grad_wq, grad_wk, grad_wv, grad_qgain, grad_kgain, grad_out, grad_mlp, grad_gate, grad_up, grad_down)
    return (output, grad_inputs, grads)

def reference(tokens, cotangent, counts, lengths, attn_gain, w_q, key_matrix, value_matrix, q_gain, k_gain, w_o, mlp_gain, w_gate, w_up, w_down):
    params = (attn_gain, w_q, key_matrix, value_matrix, q_gain, k_gain, w_o, mlp_gain, w_gate, w_up, w_down)
    grouped_query_rows = 2 * CAP
    rows_grouped = tokens.reshape(N_FSDP, grouped_query_rows, MODEL_WIDTH)
    cot_grouped = cotangent.reshape(N_FSDP, grouped_query_rows, MODEL_WIDTH)
    starting = tuple((jnp.zeros(param.shape, jnp.float32) for param in params))

    def layer_step(running, group_item):
        rows_in, cot_in, counts_row, lengths_row = group_item
        output, grad_inputs, grads = layer_group(rows_in, cot_in, counts_row, lengths_row, params)
        updated = tuple((summed + addend for summed, addend in zip(running, grads)))
        return (updated, (output, grad_inputs))
    running, stacked = lax.scan(layer_step, starting, (rows_grouped, cot_grouped, counts, lengths))
    outputs, grad_inputs = stacked
    grad_attn, grad_wq, grad_wk, grad_wv, grad_qgain, grad_kgain, grad_out, grad_mlp, grad_gate, grad_up, grad_down = running
    return (outputs.reshape(N_FSDP * grouped_query_rows, MODEL_WIDTH), grad_inputs.reshape(N_FSDP * grouped_query_rows, MODEL_WIDTH), grad_attn, grad_wq, grad_wk, grad_wv, grad_qgain, grad_kgain, grad_out, grad_mlp, grad_gate, grad_up, grad_down)
```

```python
import jax
import jax.numpy as jnp
from jax import lax
from jax.sharding import PartitionSpec as P

HEAD_SIZE = 128
EPS = 1e-06
THETA = 1000000.0
F32 = jnp.float32
BF16 = jnp.bfloat16
OWNERS = ("fsdp", "cp")


def rms_scale(x):
    return lax.rsqrt(jnp.mean(x * x, axis=-1, keepdims=True) + EPS)


def dot(left, right, ld, rd):
    return lax.dot_general(left, right, (((ld,), (rd,)), ((), ())), preferred_element_type=F32)


def bdot(left, right, ld, rd):
    return lax.dot_general(left, right, (((ld,), (rd,)), ((0,), (0,))), preferred_element_type=F32)


def shifted(x, axis, k):
    n = lax.axis_size(axis)
    return lax.ppermute(x, axis, [(i, (i + k) % n) for i in range(n)])


def tp_gather(x):
    n = lax.axis_size("tp")
    return jnp.concatenate([x] + [shifted(x, "tp", k) for k in range(1, n)], axis=0)


def tp_scatter(x, rows):
    n = lax.axis_size("tp")
    low = x.astype(BF16)
    total = x[:rows]
    for k in range(1, n):
        total = total + shifted(low[k * rows : (k + 1) * rows], "tp", -k).astype(F32)
    return total


def swap_cores(x):
    n = lax.axis_size("cp")
    return lax.ppermute(x, "cp", [(i, n - 1 - i) for i in range(n)])


def owners_gather(x):
    return lax.all_gather(x, OWNERS, axis=0, tiled=True)


def owners_scatter(x):
    return lax.psum_scatter(x, OWNERS, scatter_dimension=0, tiled=True)


def positions_of(counts_row, lengths_row, within, block):
    live = within < counts_row[block]
    pack_pos = within + jnp.where(block == 1, counts_row[0], 0)
    bounds = jnp.cumsum(lengths_row)
    seq_id = jnp.sum((bounds[None, :] <= pack_pos[:, None]).astype(jnp.int32), axis=1)
    order = jnp.arange(lengths_row.shape[0], dtype=jnp.int32)
    before = jnp.sum(jnp.where(order[None, :] < seq_id[:, None], lengths_row[None, :], 0), axis=1)
    return live, pack_pos, seq_id, pack_pos - before


def rotate(x, cosine, sine):
    half = x.shape[-1] // 2
    a, b = x[..., :half], x[..., half:]
    return jnp.concatenate([a * cosine - b * sine, b * cosine + a * sine], axis=-1)


def heads_of(x):
    return jnp.stack(
        [x[:, i : i + HEAD_SIZE] for i in range(0, x.shape[1], HEAD_SIZE)], axis=0
    )


def flat_of(x):
    return jnp.concatenate([x[i] for i in range(x.shape[0])], axis=1)


def head_norm_back(raw, gain, cosine, sine, grad):
    scale = rms_scale(raw)
    unit = raw * scale
    grad_norm = rotate(grad, cosine, -sine)
    gain_grad = jnp.sum(grad_norm * unit, axis=(0, 1))
    scaled = grad_norm * gain
    grad_raw = scale * (scaled - unit * jnp.mean(scaled * unit, axis=-1, keepdims=True))
    return grad_raw.astype(BF16), gain_grad


def row_norm_back(x, gain, grad):
    scale = rms_scale(x)
    unit = x * scale
    gain_grad = jnp.sum(grad * unit, axis=0)
    scaled = grad * gain
    return scale * (scaled - unit * jnp.mean(scaled * unit, axis=-1, keepdims=True)), gain_grad


def body(
    tokens,
    cotangent,
    counts,
    lengths,
    attn_gain,
    w_q,
    key_matrix,
    value_matrix,
    q_gain,
    k_gain,
    w_o,
    mlp_gain,
    w_gate,
    w_up,
    w_down,
):
    n_tp = lax.axis_size("tp")
    n_own = lax.axis_size("fsdp") * lax.axis_size("cp")
    tp, cp = lax.axis_index("tp"), lax.axis_index("cp")
    rows, width = tokens.shape
    n_q, n_k, n_v = w_q.shape[1], key_matrix.shape[1], value_matrix.shape[1]
    n_o, n_ff = w_o.shape[1], w_gate.shape[1]

    w_in = owners_gather(jnp.concatenate([w_q, key_matrix, value_matrix], axis=1))
    out_proj = owners_gather(w_o)
    w_mlp = owners_gather(jnp.concatenate([w_gate, w_up, w_down], axis=1))
    w_gu, down_proj = w_mlp[:, : 2 * n_ff], w_mlp[:, 2 * n_ff :]

    own_gains = jnp.concatenate([attn_gain, mlp_gain, q_gain, k_gain])
    gains = lax.all_to_all(
        jnp.broadcast_to(own_gains[None], (n_own, own_gains.shape[0])),
        OWNERS, split_axis=0, concat_axis=0, tiled=True,
    ).astype(F32)
    own_w, own_h = attn_gain.shape[0], q_gain.shape[0]
    gain_one = gains[:, :own_w].reshape(-1)
    gain_two = gains[:, own_w : 2 * own_w].reshape(-1)
    gain_q = gains[:, 2 * own_w : 2 * own_w + own_h].reshape(-1)
    gain_k = gains[:, 2 * own_w + own_h :].reshape(-1)

    block = tp_gather(tokens)
    cots = tp_gather(cotangent)

    within = jnp.concatenate(
        [((tp - k) % n_tp) * rows + jnp.arange(rows, dtype=jnp.int32) for k in range(n_tp)]
    )
    live, pos, seq, places = positions_of(counts[0], lengths[0], within, cp)
    live_b, pos_b, seq_b, _ = positions_of(counts[0], lengths[0], within, 1 - cp)
    k_live = jnp.concatenate([live, live_b])
    k_pos = jnp.concatenate([pos, pos_b])
    k_seq = jnp.concatenate([seq, seq_b])
    index = jnp.arange(within.shape[0], dtype=jnp.int32)
    k_index = jnp.arange(2 * within.shape[0], dtype=jnp.int32)
    allowed = (
        live[:, None] & k_live[None, :] & (seq[:, None] == k_seq[None, :]) & (k_pos[None, :] <= pos[:, None])
    ) | ((index[:, None] == k_index[None, :]) & jnp.logical_not(live)[:, None])
    mask_rows = live.astype(F32)[:, None]
    frequency = THETA ** (-2.0 * jnp.arange(HEAD_SIZE // 2, dtype=F32) / HEAD_SIZE)
    angles = places.astype(F32)[:, None] * frequency[None, :]
    cosine, sine = jnp.cos(angles)[None], jnp.sin(angles)[None]

    inputs = block.astype(F32) * mask_rows
    n_one = (inputs * rms_scale(inputs) * gain_one).astype(BF16)
    raw = dot(n_one, w_in, 1, 0)
    q_raw, k_raw = heads_of(raw[:, :n_q]), heads_of(raw[:, n_q : n_q + n_k])
    q = rotate(q_raw * rms_scale(q_raw) * gain_q, cosine, sine).astype(BF16)
    k_own = rotate(k_raw * rms_scale(k_raw) * gain_k, cosine, sine).astype(BF16)
    v_own = heads_of(raw[:, n_q + n_k :].astype(BF16))
    h_k = k_own.shape[0]
    kv_own = jnp.concatenate([k_own, v_own], axis=0)
    kv = jnp.concatenate([kv_own, swap_cores(kv_own)], axis=1)
    group = q.shape[0] // h_k
    keys = jnp.repeat(kv[:h_k], group, axis=0)
    values = jnp.repeat(kv[h_k:], group, axis=0)

    factor = HEAD_SIZE ** (-0.5)
    scores = jnp.where(allowed[None], bdot(q, keys, 2, 2) * factor, -jnp.inf)
    top = jnp.max(scores, axis=2, keepdims=True)
    total = top + jnp.log(jnp.sum(jnp.exp(scores - top), axis=2, keepdims=True))
    probs = jnp.exp(scores - total)
    probs_low = probs.astype(BF16)
    mixed = bdot(probs_low, values, 2, 1).astype(BF16)
    mixed_flat = flat_of(mixed)

    own_mask = mask_rows[:rows]
    own_inputs = inputs[:rows]
    residual = own_inputs + tp_scatter(dot(mixed_flat, out_proj, 1, 1), rows)
    n_two = tp_gather((residual * rms_scale(residual) * gain_two).astype(BF16))
    gate_up = dot(n_two, w_gu, 1, 0)
    gate, up = gate_up[:, :n_ff], gate_up[:, n_ff:]
    sig = jax.nn.sigmoid(gate)
    hidden = (gate * sig * up).astype(BF16)
    output = (residual + tp_scatter(dot(hidden, down_proj, 1, 1), rows)).astype(BF16)

    cot_low = (cots.astype(F32) * mask_rows).astype(BF16)
    grad_hidden = dot(cot_low, down_proj, 1, 0)
    g_down = owners_scatter(dot(cot_low, hidden, 0, 0).astype(BF16))
    d_gate = (grad_hidden * up * sig * (1.0 + gate * (1.0 - sig))).astype(BF16)
    d_up = (grad_hidden * gate * sig).astype(BF16)
    d_gu = jnp.concatenate([d_gate, d_up], axis=1)
    d_n_two = tp_scatter(dot(d_gu, w_gu, 1, 1), rows)
    g_gu = owners_scatter(dot(n_two, d_gu, 0, 0).astype(BF16))
    d_norm, part_two = row_norm_back(residual, gain_two, d_n_two)
    d_res = cotangent.astype(F32) * own_mask + d_norm
    d_res_low = tp_gather(d_res.astype(BF16))
    g_o = owners_scatter(dot(d_res_low, mixed_flat, 0, 0).astype(BF16))
    d_mixed = heads_of(dot(d_res_low, out_proj, 1, 0).astype(BF16))

    delta = jnp.sum(d_mixed.astype(F32) * mixed.astype(F32), axis=2, keepdims=True)
    d_scores = (probs * (bdot(d_mixed, values, 2, 2) - delta)).astype(BF16)
    d_q = (bdot(d_scores, keys, 2, 1) * factor).astype(BF16)

    def over_group(x):
        return jnp.sum(x.reshape(h_k, group, x.shape[1], x.shape[2]), axis=1)

    d_k = over_group(bdot(d_scores, q, 1, 1) * factor)
    d_v = over_group(bdot(probs_low, d_mixed, 1, 1))
    d_kv = jnp.concatenate([d_k, d_v], axis=0)
    half = within.shape[0]
    d_kv = (d_kv[:, :half] + swap_cores(d_kv[:, half:].astype(BF16)).astype(F32)).astype(BF16)
    dq_raw, part_q = head_norm_back(q_raw, gain_q, cosine, sine, d_q.astype(F32))
    dk_raw, part_k = head_norm_back(k_raw, gain_k, cosine, sine, d_kv[:h_k].astype(F32))
    d_in = jnp.concatenate([flat_of(dq_raw), flat_of(dk_raw), flat_of(d_kv[h_k:])], axis=1)
    g_in = owners_scatter(dot(n_one, d_in, 0, 0).astype(BF16))
    d_n_one = tp_scatter(dot(d_in, w_in, 1, 1), rows)
    d_norm, part_one = row_norm_back(own_inputs, gain_one, d_n_one)
    grad_inputs = (d_res + d_norm) * own_mask

    parts = jnp.concatenate(
        [
            part_one.reshape(n_own, -1),
            part_two.reshape(n_own, -1),
            part_q.reshape(n_own, -1),
            part_k.reshape(n_own, -1),
        ],
        axis=1,
    )
    parts = jnp.sum(
        lax.all_to_all(parts, OWNERS, split_axis=0, concat_axis=0, tiled=True), axis=0
    )
    sums = parts
    for k in range(1, n_tp):
        sums = sums + shifted(parts, "tp", k)
    g_in, g_gu = g_in.astype(F32), g_gu.astype(F32)
    return (
        output,
        grad_inputs,
        sums[:own_w],
        g_in[:, :n_q],
        g_in[:, n_q : n_q + n_k],
        g_in[:, n_q + n_k :],
        sums[2 * own_w : 2 * own_w + own_h],
        sums[2 * own_w + own_h :],
        g_o.astype(F32),
        sums[own_w : 2 * own_w],
        g_gu[:, :n_ff],
        g_gu[:, n_ff:],
        g_down.astype(F32),
    )


def solution(mesh):
    act = P(("fsdp", "cp", "tp"), None)
    pack = P("fsdp", None)
    vec = P(("fsdp", "cp"))
    mat = P(("fsdp", "cp"), "tp")
    in_specs = (act, act, pack, pack, vec, mat, mat, mat, vec, vec, mat, vec, mat, mat, mat)
    out_specs = (act, act, vec, mat, mat, mat, vec, vec, mat, vec, mat, mat, mat)
    return jax.shard_map(body, mesh=mesh, in_specs=in_specs, out_specs=out_specs, check_vma=False)
```

```python
import functools

import jax
import jax.numpy as jnp
import numpy as np
from jax import lax
from jax.experimental import pallas as pl
from jax.experimental.pallas import tpu as pltpu
from jax.sharding import PartitionSpec as P

HEAD_SIZE = 128
EPS = 1e-06
THETA = 1000000.0
RING = 8
EXTRA = 8
F32 = jnp.float32
BF16 = jnp.bfloat16


def shape_of(shape, dtype):
    return jax.ShapeDtypeStruct(tuple(shape), dtype)


def kernel_call(body, outs, *args, scalars=0, scratch=(), flops=0):
    vmem = pl.BlockSpec(memory_space=pltpu.VMEM)
    smem = pl.BlockSpec(memory_space=pltpu.SMEM)
    size = sum(a.size * a.dtype.itemsize for a in (*args, *outs))
    return pl.pallas_call(
        body,
        out_shape=outs,
        in_specs=[smem] * scalars + [vmem] * (len(args) - scalars),
        out_specs=[vmem] * len(outs),
        scratch_shapes=list(scratch),
        cost_estimate=pl.CostEstimate(flops=flops, bytes_accessed=size, transcendentals=0),
    )(*args)


def rms_scale(x):
    return lax.rsqrt(jnp.mean(x * x, axis=-1, keepdims=True) + EPS)


def dot(left, right, ld, rd):
    return lax.dot_general(left, right, (((ld,), (rd,)), ((), ())), preferred_element_type=F32)


def fill(target, pieces):
    at = 0
    for piece in pieces:
        target[at : at + piece.shape[0], :] = piece[...]
        at += piece.shape[0]


def send_parts(part, own, sends):
    rows = own.shape[0]
    own[...] = part[:rows, :]
    for k, ref in enumerate(sends):
        ref[...] = part[(k + 1) * rows : (k + 2) * rows, :].astype(BF16)


def spin(x, cosine, sine):
    return x * cosine + pltpu.roll(x, HEAD_SIZE // 2, 1) * sine


def head(i):
    return slice(i * HEAD_SIZE, (i + 1) * HEAD_SIZE)


def tiles(total, size, step):
    def run(i, carry):
        step(pl.ds(pl.multiple_of(i * size, size), size))
        return carry

    lax.fori_loop(0, total // size, run, 0)


def join_kernel(*refs):
    at = 0
    for ref in refs[:-1]:
        refs[-1][:, at : at + ref.shape[1]] = ref[...]
        at += ref.shape[1]


def owner_of(i):
    n, z, c = lax.axis_size("fsdp"), lax.axis_index("fsdp"), lax.axis_index("cp")
    return lax.rem(z - i % n + n, n) * 2 + (c if i < n else 1 - c)


def lanes(i, own):
    return pl.ds(pl.multiple_of(owner_of(i) * own, own), own)


def pack_kernel(own, gate, up, down, x, e, both, x_out, e_out):
    join_kernel(gate, up, down, both)
    for i in range(x.shape[1] // own):
        to = slice(i * own, (i + 1) * own)
        x_out[:, to] = x[:, lanes(i, own)]
        e_out[:, to] = e[:, lanes(i, own)]


def place_kernel(rows, counts, lengths, frequency, mask, low, high, k_pos, cosine, sine):
    n, t, c = lax.axis_size("tp"), lax.axis_index("tp"), lax.axis_index("cp")
    cap = n * rows

    def places(within, block):
        live = within < counts[0, block]
        place = within + jnp.where(block == 1, counts[0, 0], 0)
        start, bound = jnp.zeros_like(place), 0
        for i in range(lengths.shape[1]):
            bound = bound + lengths[0, i]
            start = jnp.where(place >= bound, bound, start)
        apart = (4 + block) * cap + within
        return live, place, start, jnp.where(live, place, apart), jnp.where(live, start, apart)

    sign = jnp.where(lax.broadcasted_iota(jnp.int32, (1, HEAD_SIZE), 1) < HEAD_SIZE // 2, -1.0, 1.0)
    for k in range(n):
        at = slice(k * rows, (k + 1) * rows)
        first = lax.rem(t - k + n, n) * rows
        within = first + lax.broadcasted_iota(jnp.int32, (rows, HEAD_SIZE), 0)
        live, place, start, last, begin = places(within, c)
        mask[at, :] = live.astype(F32)[:, :1]
        low[at, :] = begin[:, :1]
        high[at, :] = last[:, :1]
        angles = (place - start).astype(F32) * frequency[0:1, :]
        cosine[at, :] = jnp.cos(angles)
        sine[at, :] = jnp.sin(angles) * sign
        within = first + lax.broadcasted_iota(jnp.int32, (EXTRA, rows), 1)
        k_pos[:, at] = places(within, c)[3]
        k_pos[:, cap + k * rows : cap + (k + 1) * rows] = places(within, 1 - c)[3]


def branch_kernel(n_send, tile, hidden, w, own, *refs):
    sends, (part,) = refs[:n_send], refs[n_send:]

    def step(t):
        part[t, :] = dot(hidden[t, :], w[...], 1, 1)

    tiles(hidden.shape[0], tile, step)
    send_parts(part, own, sends)


def norm_kernel(*refs):
    x, mask, gain, part, *terms = refs[:-2]
    residual, n = refs[-2:]
    h = x[...].astype(F32) * mask[: x.shape[0], :] + part[...]
    for term in terms:
        h = h + term[...].astype(F32)
    residual[...] = h
    n[...] = (h * rms_scale(h) * gain[1:2, :]).astype(BF16)


def norm_back_of(x, gain, grad):
    scale = rms_scale(x)
    unit = x * scale
    scaled = grad * gain
    out = scale * (scaled - unit * jnp.mean(scaled * unit, axis=1, keepdims=True))
    return out, grad * unit


def norm_back_kernel(*refs):
    e, mask, gain, residual, part, *terms = refs[:-3]
    d_res, sent, sums = refs[-3:]
    grad = part[...]
    for term in terms:
        grad = grad + term[...].astype(F32)
    back, unit = norm_back_of(residual[...], gain[1:2, :], grad)
    back = e[...].astype(F32) * mask[: e.shape[0], :] + back
    d_res[...] = back
    rows = back.shape[0]
    sent[:rows, :] = back.astype(BF16)
    line = jnp.sum(unit, axis=0, keepdims=True)
    sums[...] = jnp.broadcast_to(line, sums.shape)
    sent[rows:, :] = jnp.broadcast_to(line, sums.shape).astype(BF16)


def out_kernel(own, *refs):
    residual, branch, *terms = refs[:-1]
    y = residual[...] + branch[...]
    for term in terms:
        y = y + term[...].astype(F32)
    y = y.astype(BF16)
    if own is None:
        refs[-1][...] = y
        return
    for i in range(y.shape[1] // own):
        refs[-1][:, lanes(i, own)] = y[:, i * own : (i + 1) * own]


def input_back_kernel(own, *refs):
    x, mask, gain, d_res, part, line, two, *terms = refs[:-2]
    out, sums = refs[-2:]
    rows = part.shape[0]
    grad, total = part[...], line[...]
    for term in terms:
        grad = grad + term[:rows, :].astype(F32)
        total = total + term[rows:, :].astype(F32)
    live = mask[:rows, :]
    back, _ = norm_back_of(x[...].astype(F32) * live, gain[0:1, :], grad)
    y = (d_res[...] + back) * live
    if own is None:
        out[...] = y
        sums[...] = total
        return
    per = HEAD_SIZE * own // y.shape[1]
    for i in range(y.shape[1] // own):
        at = slice(i * own, (i + 1) * own)
        out[:, lanes(i, own)] = y[:, at]
        turn = lax.rem(HEAD_SIZE - owner_of(i) * per, HEAD_SIZE)
        sums[i : i + 1, :own] = total[0:1, at]
        sums[i : i + 1, own : 2 * own] = two[0:1, at]
        sums[i : i + 1, 2 * own : 2 * own + HEAD_SIZE] = pltpu.roll(total[1:2, head(0)], turn, 1)
        sums[i : i + 1, 2 * own + HEAD_SIZE :] = pltpu.roll(total[1:2, head(1)], turn, 1)


def qkv_kernel(n_x, n_w, n_q, n_k, tile, *refs):
    xs, rest = refs[:n_x], refs[n_x:]
    ws, rest = rest[:n_w], rest[n_w:]
    mask, cosine, sine, gains, x0, n_one, raw, q, kv, w = rest
    fill(w, ws)
    fill(x0, xs)
    gain, gain_q, gain_k = gains[0:1, :], gains[2:3, head(0)], gains[2:3, head(1)]

    def step(t):
        x = x0[t, :].astype(F32) * mask[t, :]
        x0[t, :] = x.astype(BF16)
        n = (x * rms_scale(x) * gain).astype(BF16)
        n_one[t, :] = n
        out = dot(n, w[...], 1, 0)
        raw[t, :] = out[:, : n_q + n_k]
        c, s = cosine[t, :], sine[t, :]
        for i in range(n_q // HEAD_SIZE):
            u = out[:, head(i)]
            q[t, head(i)] = spin(u * rms_scale(u) * gain_q, c, s).astype(BF16)
        for i in range(n_k // HEAD_SIZE):
            u = out[:, n_q + i * HEAD_SIZE : n_q + (i + 1) * HEAD_SIZE]
            kv[t, head(i)] = spin(u * rms_scale(u) * gain_k, c, s).astype(BF16)
        kv[t, n_k:] = out[:, n_q + n_k :].astype(BF16)

    tiles(x0.shape[0], tile, step)


def attend_kernel(tile, q, kv_own, kv_other, low, high, k_pos, probs, mixed, kv):
    fill(kv, (kv_own, kv_other))
    heads = q.shape[1] // HEAD_SIZE
    h_k = kv.shape[1] // HEAD_SIZE // 2
    factor = HEAD_SIZE ** (-0.5)

    def step(t):
        allowed = (k_pos[0:1, :] >= low[t, :]) & (k_pos[0:1, :] <= high[t, :])
        for i in range(heads):
            g = i * h_k // heads
            s = jnp.where(allowed, dot(q[t, head(i)], kv[:, head(g)], 1, 1) * factor, -jnp.inf)
            e = jnp.exp(s - jnp.max(s, axis=1, keepdims=True))
            p = (e * (1.0 / jnp.sum(e, axis=1, keepdims=True))).astype(BF16)
            probs[i, t, :] = p
            mixed[t, head(i)] = dot(p, kv[:, head(h_k + g)], 1, 0).astype(BF16)

    tiles(q.shape[0], tile, step)


def out_proj_kernel(n_w, n_send, tile, mixed, *refs):
    ws, rest = refs[:n_w], refs[n_w:]
    w, own = rest[:2]
    sends, (part,) = rest[2 : 2 + n_send], rest[2 + n_send :]
    fill(w, ws)

    def step(t):
        part[t, :] = dot(mixed[t, :], w[...], 1, 1)

    tiles(mixed.shape[0], tile, step)
    send_parts(part, own, sends)


def mlp_join_kernel(n_x, n_ff, *refs):
    cs, ws = refs[:n_x], refs[n_x:-4]
    mask, cot, w_gu, w_down = refs[-4:]
    fill(w_gu, [w.at[:, : 2 * n_ff] for w in ws])
    fill(w_down, [w.at[:, 2 * n_ff :] for w in ws])
    rows = cs[0].shape[0]
    for k, c in enumerate(cs):
        at = slice(k * rows, (k + 1) * rows)
        cot[at, :] = (c[...].astype(F32) * mask[at, :]).astype(BF16)


def mlp_kernel(n_x, n_send, tile, *refs):
    xs, refs = refs[:n_x], refs[n_x:]
    cot, w_gu, w_down, n_two, hidden, d_gu, own = refs[:7]
    sends, (part,) = refs[7 : 7 + n_send], refs[7 + n_send :]
    n_ff = hidden.shape[1]
    fill(n_two, xs)

    def step(t):
        both = dot(n_two[t, :], w_gu[...], 1, 0)
        gate, up = both[:, :n_ff], both[:, n_ff:]
        dz = dot(cot[t, :], w_down[...], 1, 0)
        sig = 1.0 / (1.0 + jnp.exp(-gate))
        act = gate * sig
        hidden[t, :] = (act * up).astype(BF16)
        d_gu[t, :n_ff] = (dz * up * sig * (1.0 + gate * (1.0 - sig))).astype(BF16)
        d_gu[t, n_ff:] = (dz * act).astype(BF16)

    tiles(n_two.shape[0], tile, step)
    part[...] = dot(d_gu[...], w_gu[...], 1, 1)
    send_parts(part, own, sends)


def attend_back_kernel(n_x, tile, *refs):
    xs, refs = refs[:n_x], refs[n_x:]
    probs, mixed, q, kv_own, kv_other, w, d_res, d_q, d_own, d_other, kv, da, acc = refs
    rows, half = xs[0].shape[0] - EXTRA, kv_own.shape[0]
    for k, x in enumerate(xs):
        d_res[k * rows : (k + 1) * rows, :] = x[:rows, :]
    fill(kv, (kv_own, kv_other))
    heads = q.shape[1] // HEAD_SIZE
    h_k = kv.shape[1] // HEAD_SIZE // 2
    factor = HEAD_SIZE ** (-0.5)
    acc[...] = jnp.zeros_like(acc)

    def step(t):
        da[t, :] = dot(d_res[t, :], w[...], 1, 0).astype(BF16)
        for i in range(heads):
            g = i * h_k // heads
            d = da[t, head(i)]
            delta = jnp.sum(d.astype(F32) * mixed[t, head(i)].astype(F32), axis=1, keepdims=True)
            p = probs[i, t, :]
            ds = (p.astype(F32) * (dot(d, kv[:, head(h_k + g)], 1, 1) - delta)).astype(BF16)
            d_q[t, head(i)] = (dot(ds, kv[:, head(g)], 1, 0) * factor).astype(BF16)
            acc[:, head(g)] += dot(ds, q[t, head(i)], 0, 0) * factor
            acc[:, head(h_k + g)] += dot(p, d, 0, 0)

    tiles(q.shape[0], tile, step)
    d_own[...] = acc[:half, :]
    d_other[...] = acc[half:, :].astype(BF16)


def qkv_back_kernel(n_send, n_q, n_k, tile, *refs):
    d_q, d_own, d_got, raw, x0, cosine, sine, gains, w = refs[:9]
    d_in, own = refs[9:11]
    sends, (sums, part) = refs[11 : 11 + n_send], refs[11 + n_send :]
    gain_q, gain_k = gains[2:3, head(0)], gains[2:3, head(1)]
    sums[...] = jnp.zeros_like(sums)

    def back(u, gain, grad, c, s):
        scale = rms_scale(u)
        unit = u * scale
        grad = spin(grad, c, s)
        scaled = grad * gain
        out = scale * (scaled - unit * jnp.mean(scaled * unit, axis=1, keepdims=True))
        return out.astype(BF16), jnp.sum(grad * unit, axis=0, keepdims=True)

    def step(t):
        c, s = cosine[t, :], -sine[t, :]
        total = jnp.zeros((1, HEAD_SIZE), F32)
        for i in range(n_q // HEAD_SIZE):
            out, term = back(raw[t, head(i)], gain_q, d_q[t, head(i)].astype(F32), c, s)
            d_in[t, head(i)] = out
            total += term
        sums[1:2, head(0)] += total
        total = jnp.zeros((1, HEAD_SIZE), F32)
        d_kv = (d_own[t, :] + d_got[t, :].astype(F32)).astype(BF16)
        for i in range(n_k // HEAD_SIZE):
            at = slice(n_q + i * HEAD_SIZE, n_q + (i + 1) * HEAD_SIZE)
            out, term = back(raw[t, at], gain_k, d_kv[:, head(i)].astype(F32), c, s)
            d_in[t, at] = out
            total += term
        sums[1:2, head(1)] += total
        d_in[t, n_q + n_k :] = d_kv[:, n_k:]

    def sum_step(t):
        x = x0[t, :].astype(F32)
        sums[0:1, :] += jnp.sum(part[t, :] * (x * rms_scale(x)), axis=0, keepdims=True)

    tiles(x0.shape[0], tile, step)
    part[...] = dot(d_in[...], w[...], 1, 1)
    tiles(x0.shape[0], tile, sum_step)
    rows = own.shape[0]
    own[...] = part[:rows, :]
    for k, ref in enumerate(sends):
        ref[:rows, :] = part[(k + 1) * rows : (k + 2) * rows, :].astype(BF16)
        ref[rows:, :] = sums[...].astype(BF16)


def shifted(x, axis, k):
    n = lax.axis_size(axis)
    return lax.ppermute(x, axis, [(i, (i + k) % n) for i in range(n)])


def tp_parts(x):
    return [x] + [shifted(x, "tp", k) for k in range(1, lax.axis_size("tp"))]


def tp_terms(sends):
    return [shifted(x, "tp", -k - 1) for k, x in enumerate(sends)]


def swap_cores(x):
    n = lax.axis_size("cp")
    return lax.ppermute(x, "cp", [(i, n - 1 - i) for i in range(n)])


def pieces_of(x):
    n, z = lax.axis_size("fsdp"), lax.axis_index("fsdp")
    if n > RING:
        whole = lax.all_gather(x, "fsdp", axis=0)
        whole = whole[(z - jnp.arange(n)) % n].reshape(n * x.shape[0], x.shape[1])
        return [jnp.concatenate([whole, swap_cores(whole)], axis=0)]
    chain = [x]
    for _ in range(1, n):
        chain.append(shifted(chain[-1], "fsdp", 1))
    return [*chain, *(swap_cores(y) for y in chain)]


def owners_sum(act, grad, own, parts=None):
    n, z = lax.axis_size("fsdp"), lax.axis_index("fsdp")
    half, width = act.shape[1] // 2, grad.shape[1]
    parts = parts or (width,)
    there = dot(act[:, half:], grad, 0, 0).astype(BF16)
    there = swap_cores(there)
    here = dot(act[:, :half], grad, 0, 0) + there.astype(F32)
    if n > RING:
        ordered = here.reshape(n, own, -1)[(z - jnp.arange(n)) % n].astype(BF16)
        total = lax.psum_scatter(ordered, "fsdp", scatter_dimension=0, tiled=False).astype(F32)
        return jnp.split(total, np.cumsum(parts)[:-1], axis=1)
    blocks = [here[s * own : (s + 1) * own] for s in range(n)]
    total = blocks[1 % n]
    for s in range(2, n + 1):
        got = shifted(total.astype(BF16), "fsdp", 1)
        total = blocks[s % n] + got.astype(F32)
    return jnp.split(total, np.cumsum(parts)[:-1], axis=1)


def layer(
    tokens,
    cotangent,
    counts,
    lengths,
    attn_gain,
    w_q,
    key_matrix,
    value_matrix,
    q_gain,
    k_gain,
    w_o,
    mlp_gain,
    w_gate,
    w_up,
    w_down,
):
    n_tp, n_z = lax.axis_size("tp"), lax.axis_size("fsdp")
    cp, z = lax.axis_index("cp"), lax.axis_index("fsdp")
    rows, width = tokens.shape
    n_q, n_k, n_v = w_q.shape[1], key_matrix.shape[1], value_matrix.shape[1]
    n_in, n_o, n_ff = n_q + n_k + n_v, w_o.shape[1], w_gate.shape[1]
    own, own_h = w_q.shape[0], q_gain.shape[0]
    cap = n_tp * rows
    tile = cap // 2

    wide = own % HEAD_SIZE == 0
    steps = [(z - s + n_z) % n_z for s in range(n_z)]
    place = [2 * s + cp for s in steps] + [2 * s + 1 - cp for s in steps]
    where = [jnp.where(i % 2 == cp, 0, n_z) + (z - i // 2 + n_z) % n_z for i in range(2 * n_z)]

    def moved(x, order):
        return jnp.concatenate(
            [lax.dynamic_slice_in_dim(x, order[i] * own, own, axis=1) for i in range(2 * n_z)], axis=1
        )

    (a0,) = kernel_call(join_kernel, [shape_of((own, n_in), BF16)], w_q, key_matrix, value_matrix)
    flat = [shape_of((rows, width), BF16)] * 2
    if wide:
        c0, tokens, cotangent = kernel_call(
            functools.partial(pack_kernel, own), [shape_of((own, 3 * n_ff), BF16), *flat],
            w_gate, w_up, w_down, tokens, cotangent,
        )
    else:
        c0 = jnp.concatenate([w_gate, w_up, w_down], axis=1)
        tokens, cotangent = moved(tokens, place), moved(cotangent, place)
    line = jnp.concatenate([attn_gain, mlp_gain, q_gain, k_gain])
    p_in, p_out, p_mlp = (pieces_of(x) for x in (a0, w_o, c0))
    if n_z > RING:
        gains = pieces_of(line[None])[0].astype(F32)
    else:
        lines = ([line] + [shifted(line, "fsdp", s) for s in range(1, n_z)])
        lines = jnp.stack(lines)
        gains = jnp.concatenate([lines, swap_cores(lines)], axis=0).astype(F32)

    def arranged(x, order):
        return jnp.concatenate(
            [lax.dynamic_slice_in_dim(x, order[i], 1, axis=0) for i in range(2 * n_z)], axis=0
        )

    gain_one = gains[:, :own].reshape(1, -1)
    gain_two = gains[:, own : 2 * own].reshape(1, -1)
    gain_qk = arranged(gains[:, 2 * own :], where)
    gain_qk = jnp.concatenate(
        [gain_qk[:, :own_h].reshape(1, -1), gain_qk[:, own_h:].reshape(1, -1), jnp.zeros((1, width - 2 * HEAD_SIZE), F32)],
        axis=1,
    )
    gain_rows = jnp.concatenate([gain_one, gain_two, gain_qk, jnp.zeros((EXTRA - 3, width), F32)], axis=0)

    x_parts, cot_parts = tp_parts(tokens), tp_parts(cotangent)

    lane = np.arange(HEAD_SIZE) % (HEAD_SIZE // 2)
    frequency = (THETA ** (-2.0 * lane / HEAD_SIZE)).astype(np.float32)
    mask, low, high, k_pos, cosine, sine = kernel_call(
        functools.partial(place_kernel, rows),
        [
            shape_of((cap, 1), F32),
            shape_of((cap, 1), jnp.int32),
            shape_of((cap, 1), jnp.int32),
            shape_of((EXTRA, 2 * cap), jnp.int32),
            shape_of((cap, HEAD_SIZE), F32),
            shape_of((cap, HEAD_SIZE), F32),
        ],
        counts, lengths, jnp.broadcast_to(jnp.asarray(frequency)[None], (EXTRA, HEAD_SIZE)),
        scalars=2,
    )

    n_w, n_send = len(p_in), n_tp - 1
    sends = [shape_of((rows, width), BF16)] * n_send
    own_part = shape_of((rows, width), F32)
    x0, n_one, raw, q, kv, w_in = kernel_call(
        functools.partial(qkv_kernel, n_tp, n_w, n_q, n_k, tile),
        [
            shape_of((cap, width), BF16),
            shape_of((cap, width), BF16),
            shape_of((cap, n_q + n_k), F32),
            shape_of((cap, n_q), BF16),
            shape_of((cap, n_k + n_v), BF16),
            shape_of((width, n_in), BF16),
        ],
        *x_parts, *p_in, mask, cosine, sine, gain_rows,
        flops=2 * cap * width * n_in,
    )
    kv_other = swap_cores(kv)
    heads = n_q // HEAD_SIZE
    probs, mixed = kernel_call(
        functools.partial(attend_kernel, tile),
        [shape_of((heads, cap, 2 * cap), BF16), shape_of((cap, n_q), BF16)],
        q, kv, kv_other, low, high, k_pos,
        scratch=[pltpu.VMEM((2 * cap, n_k + n_v), BF16)],
        flops=8 * cap * cap * n_q,
    )
    out_proj, part, *to_send = kernel_call(
        functools.partial(out_proj_kernel, n_w, n_send, cap),
        [shape_of((width, n_o), BF16), own_part, *sends],
        mixed, *p_out,
        scratch=[pltpu.VMEM((cap, width), F32)],
        flops=2 * cap * n_q * width,
    )
    residual, normed = kernel_call(
        norm_kernel, [own_part, flat[0]],
        tokens, mask, gain_rows, part, *tp_terms(to_send),
    )
    n_parts = tp_parts(normed)

    cots, w_gu, down_proj = kernel_call(
        functools.partial(mlp_join_kernel, n_tp, n_ff),
        [shape_of((cap, width), BF16), shape_of((width, 2 * n_ff), BF16), shape_of((width, n_ff), BF16)],
        *cot_parts, *p_mlp, mask,
    )
    n_two, hidden, d_gu, part, *to_send = kernel_call(
        functools.partial(mlp_kernel, n_tp, n_send, tile),
        [
            shape_of((cap, width), BF16),
            shape_of((cap, n_ff), BF16),
            shape_of((cap, 2 * n_ff), BF16),
            own_part,
            *sends,
        ],
        *n_parts, cots, w_gu, down_proj,
        scratch=[pltpu.VMEM((cap, width), F32)],
        flops=10 * cap * width * n_ff,
    )
    branch, *outs = kernel_call(
        functools.partial(branch_kernel, n_send, cap), [own_part, *sends], hidden, down_proj,
        scratch=[pltpu.VMEM((cap, width), F32)],
        flops=2 * cap * width * n_ff,
    )
    d_res, sent, part_two = kernel_call(
        norm_back_kernel,
        [own_part, shape_of((rows + EXTRA, width), BF16), shape_of((EXTRA, width), F32)],
        cotangent, mask, gain_rows, residual, part, *tp_terms(to_send),
    )
    (g_down,) = owners_sum(cots, hidden, own)
    g_gate, g_up = owners_sum(n_two, d_gu, own, (n_ff, n_ff))
    got = tp_parts(sent)
    (output,) = kernel_call(
        functools.partial(out_kernel, own if wide else None), [flat[0]],
        residual, branch, *tp_terms(outs),
    )
    part_two = part_two + sum(x[rows:].astype(F32) for x in got[1:])
    d_low, d_q, d_own, d_other = kernel_call(
        functools.partial(attend_back_kernel, n_tp, tile),
        [
            shape_of((cap, width), BF16),
            shape_of((cap, n_q), BF16),
            shape_of((cap, n_k + n_v), F32),
            shape_of((cap, n_k + n_v), BF16),
        ],
        *got, probs, mixed, q, kv, kv_other, out_proj,
        scratch=[
            pltpu.VMEM((2 * cap, n_k + n_v), BF16),
            pltpu.VMEM((cap, n_q), BF16),
            pltpu.VMEM((2 * cap, n_k + n_v), F32),
        ],
        flops=16 * cap * cap * n_q + 2 * cap * n_q * width,
    )
    (g_o,) = owners_sum(d_low, mixed, own)
    d_in, part, *to_send = kernel_call(
        functools.partial(qkv_back_kernel, n_send, n_q, n_k, tile),
        [
            shape_of((cap, n_in), BF16),
            own_part,
            *([shape_of((rows + EXTRA, width), BF16)] * n_send),
            shape_of((EXTRA, width), F32),
        ],
        d_q, d_own, swap_cores(d_other), raw, x0, cosine, sine, gain_rows, w_in,
        scratch=[pltpu.VMEM((cap, width), F32)],
        flops=2 * cap * width * n_in,
    )
    to_send, line = to_send[:-1], to_send[-1]
    g_q, g_k, g_v = owners_sum(n_one, d_in, own, (n_q, n_k, n_v))
    sums_shape = (2 * n_z, 2 * own + 2 * HEAD_SIZE) if wide else (EXTRA, width)
    grad_inputs, sums = kernel_call(
        functools.partial(input_back_kernel, own if wide else None),
        [own_part, shape_of(sums_shape, F32)],
        tokens, mask, gain_rows, d_res, part, line, part_two, *tp_terms(to_send),
    )
    if wide:
        at_q, at_k = 2 * own, 2 * own + HEAD_SIZE
    else:
        at_q, at_k = 2 * own, 2 * own + own_h
        output, grad_inputs = moved(output, where), moved(grad_inputs, where)
        part_qk = [sums[1, head(i)].reshape(2 * n_z, -1) for i in range(2)]
        sums = jnp.concatenate(
            [
                sums[0].reshape(2 * n_z, -1),
                part_two[0].reshape(2 * n_z, -1),
                arranged(jnp.concatenate(part_qk, axis=1), place),
            ],
            axis=1,
        )
    sums = sums[:n_z] + swap_cores(sums[n_z:])
    if n_z > RING:
        sums = lax.psum_scatter(sums[jnp.stack(steps)], "fsdp", scatter_dimension=0, tiled=False)
    else:
        sums = sums[0] + sum(shifted(sums[s], "fsdp", -s) for s in range(1, n_z))
    return (
        output,
        grad_inputs,
        sums[:own],
        g_q,
        g_k,
        g_v,
        sums[at_q : at_q + own_h],
        sums[at_k : at_k + own_h],
        g_o,
        sums[own : 2 * own],
        g_gate,
        g_up,
        g_down,
    )


def solution(mesh):
    act = P(("fsdp", "cp", "tp"), None)
    pack = P("fsdp", None)
    vec = P(("fsdp", "cp"))
    mat = P(("fsdp", "cp"), "tp")
    in_specs = (act, act, pack, pack, vec, mat, mat, mat, vec, vec, mat, vec, mat, mat, mat)
    out_specs = (act, act, vec, mat, mat, mat, vec, vec, mat, vec, mat, mat, mat)
    return jax.shard_map(layer, mesh=mesh, in_specs=in_specs, out_specs=out_specs, check_vma=False)
```
